32 devices in a mesh: grid: 4 (over y, x), comp: 8 (over z, core).
Axes of the slice: x: 2, y: 2, z: 4, core: 2. Of those that a mesh axis runs over, the one named last changes fastest.
Arguments:
- spectrum: bfloat16 [4, 1152, 4096], P('grid', 'comp'), may hold values from -6 to 6
- sea_mask: int32 [4, 4096], P('grid'), may hold values 0 or 1
- speed: float32 [4, 32], P('grid'), may hold values from 0.05 to 0.95
- coupling_a: bfloat16 [1152, 1152], replicated, may hold values from -0.1875 to 0.1875
- coupling_b: bfloat16 [1152, 1152], replicated, may hold values from -0.1875 to 0.1875
- send_index: int32 [4, 8, 4, 16], P('grid', 'comp'), may hold values from 0 to 511
- recv_index: int32 [4, 8, 64], P('grid', 'comp'), may hold values from 0 to 511
- recv_weight: float32 [4, 8, 64], P('grid', 'comp'), may hold values from 0.3 to 3
Outputs:
- final_spectrum: bfloat16 [4, 1152, 4096], P('grid', 'comp')
The draws below stay inside these ranges and needn't reach their ends.
All inputs are finite; a program needn't handle non-finite values. No bound on the sum of `sea_mask` on one device may be relied on, other than what follows from the above.
Results may differ from the reference program's by a relative error of at most 0.0067.
Values may be sent and summed in bfloat16 or wider, within the bound.
A program may use at most 64 MiB of HBM per device.

```python
import math
import jax
import jax.numpy as jnp
from jax import lax

ND = 36
NF = 32
PTS_DEV = 512
LX = 128
OVB = 16
STEPS = 2
K = 1152
P_SIZE = 4096
N_GRID = 4
N_COMP = 8


def place_ends(entries, stream_key, smallest, largest):
    place = [jax.random.randint(jax.random.fold_in(stream_key, axis), (), 0, length) for axis, length in enumerate(entries.shape)]
    widest = entries.shape.index(max(entries.shape))
    next_to = place[:widest] + [(place[widest] + 1) % entries.shape[widest]] + place[widest + 1:]
    return entries.at[tuple(place)].set(smallest).at[tuple(next_to)].set(largest)


def steps_of(own_key, shape, cuts, smallest, top_value):
    def one(position, blocks):
        draws = jax.random.uniform(jax.random.fold_in(jax.random.fold_in(own_key, 6), position), (blocks,), jnp.float32, smallest / len(cuts), top_value / len(cuts))
        return jnp.repeat(jnp.exp(draws), shape[position] // blocks).reshape((-1,) + (1,) * (len(shape) - position - 1))

    gain = one(*cuts[0])
    for cut in cuts[1:]:
        gain = gain * one(*cut)
    return gain


def normal_values(stream_key, dims, spread, reach, split=(), kind=jnp.bfloat16):
    drawn = jax.random.normal(stream_key, dims, jnp.float32) * spread
    if len(split) > 0:
        drawn = steps_of(stream_key, dims, split, -0.22, 0.18) * drawn
    return jnp.clip(drawn, min=-reach, max=reach).astype(kind)


def setup_inputs(seed: int = 0) -> dict:
    keys = jax.random.split(jax.random.key(seed), 9)
    spectrum = normal_values(keys[0], (N_GRID, K, P_SIZE), 1.0, 6.0, ((0, 4), (1, 8)))
    sea_mask = place_ends((jax.random.randint(keys[1], (N_GRID, P_SIZE), 0, 5) < 4).astype(jnp.int32), jax.random.fold_in(keys[1], 1), 0, 1)
    speed = jnp.clip(jnp.exp(math.log(0.95) - 2.944439 * jax.random.uniform(keys[2], (N_GRID, NF), jnp.float32) ** steps_of(keys[2], (N_GRID, NF), ((0, 4),), -0.2, 0.2)), 0.05, 0.95)
    coupling_a = normal_values(keys[3], (K, K), K ** -0.5, 0.1875)
    coupling_b = normal_values(keys[4], (K, K), K ** -0.5, 0.1875)
    send_index = place_ends(jax.random.randint(keys[5], (N_GRID, N_COMP, N_GRID, OVB), 0, PTS_DEV), jax.random.fold_in(keys[5], 1), 0, PTS_DEV - 1).astype(jnp.int32)
    recv_index = place_ends(jax.random.randint(keys[6], (N_GRID, N_COMP, N_GRID * OVB), 0, PTS_DEV), jax.random.fold_in(keys[6], 1), 0, PTS_DEV - 1).astype(jnp.int32)
    recv_weight = jnp.clip(jnp.exp(math.log(3.0) - 2.3025851 * jax.random.uniform(keys[7], (N_GRID, N_COMP, N_GRID * OVB), jnp.float32) ** steps_of(keys[7], (N_GRID, N_COMP, N_GRID * OVB), ((0, 4), (1, 8)), -0.2, 0.2)), 0.3, 3.0)
    return dict(spectrum=spectrum, sea_mask=sea_mask, speed=speed, coupling_a=coupling_a, coupling_b=coupling_b, send_index=send_index, recv_index=recv_index, recv_weight=recv_weight)


def courant(comp_index, speed_row):
    direction = comp_index // NF
    frequency = comp_index % NF
    heading = 2.0 * math.pi * direction.astype(jnp.float32) / ND
    onehot_table = (frequency[:, None] == jnp.arange(NF, dtype=jnp.int32)[None, :]).astype(jnp.float32)
    celerity = jnp.sum(onehot_table * speed_row[None, :], axis=1)
    return celerity * jnp.cos(heading), celerity * jnp.sin(heading)


def sweep_columns(values, number):
    padded = jnp.pad(values, ((0, 0), (0, 0), (1, 1)))
    forward = padded[:, :, 2:]
    behind = padded[:, :, :-2]
    return values - 0.5 * number * (forward - behind) + 0.5 * number * number * (forward - 2.0 * values + behind)


def sweep_rows(values, number):
    padded = jnp.pad(values, ((0, 0), (1, 1), (0, 0)))
    forward = padded[:, 2:, :]
    behind = padded[:, :-2, :]
    return values - 0.5 * number * (forward - behind) + 0.5 * number * number * (forward - 2.0 * values + behind)


def propagate(spectra, sea_float, courant_x, courant_y):
    count = spectra.shape[0]
    values = spectra.astype(jnp.float32).reshape(count, -1, LX)
    land_sea = sea_float.reshape(1, -1, LX)
    values = sweep_columns(values, courant_x[:, None, None]) * land_sea
    values = sweep_rows(values, courant_y[:, None, None]) * land_sea
    return values.reshape(count, -1).astype(jnp.bfloat16)


def source(points, sea_part, coupling_a, coupling_b):
    first_term = jnp.dot(coupling_a, points, preferred_element_type=jnp.float32)
    second = jnp.dot(coupling_b, points, preferred_element_type=jnp.float32)
    return (points.astype(jnp.float32) + 0.5 * sea_part[None, :] * first_term * jnp.tanh(second)).astype(jnp.bfloat16)


def average(updated, received, targets, weights):
    count = updated.shape[1]
    hits = targets[:, None] == jnp.arange(count, dtype=jnp.int32)[None, :]
    weighted = (received.astype(jnp.float32) * weights[:, None]).astype(jnp.bfloat16)
    onehot_table = hits.astype(jnp.bfloat16)
    gathered_sum = lax.dot_general(weighted, onehot_table, (((0,), (0,)), ((), ())), preferred_element_type=jnp.float32)
    numerator = updated.astype(jnp.float32) + gathered_sum
    denominator = 1.0 + jnp.sum(hits.astype(jnp.float32) * weights[:, None], axis=0)
    return (numerator / denominator[None, :]).astype(jnp.bfloat16)


def pick_block(block_data, picks):
    return jnp.take(block_data, picks, axis=1).T


def reference(spectrum, sea_mask, speed, coupling_a, coupling_b, send_index, recv_index, recv_weight):
    total_comps = ND * NF
    comp_all = jnp.arange(total_comps, dtype=jnp.int32)
    sea_float = sea_mask.astype(jnp.float32)

    def courant_grid(speed_row):
        return courant(comp_all, speed_row)

    courant_x, courant_y = jax.vmap(courant_grid)(speed)

    def propagate_grid(items):
        return propagate(items[0], items[1], items[2], items[3])

    def source_grid(items):
        return source(items[0], items[1], coupling_a, coupling_b)

    def average_grid(items):
        return jax.vmap(average)(items[0], items[1], items[2], items[3])

    spectra = spectrum
    for turn_index in range(STEPS):
        advected = lax.map(propagate_grid, (spectra, sea_float, courant_x, courant_y))
        updated = lax.map(source_grid, (advected, sea_float))
        blocks = updated.reshape(N_GRID, total_comps, N_COMP, PTS_DEV).transpose(0, 2, 1, 3)
        picked = jax.vmap(jax.vmap(pick_block))(blocks, send_index.reshape(N_GRID, N_COMP, N_GRID * OVB))
        forwarded = picked.reshape(N_GRID, N_COMP, N_GRID, OVB, total_comps).transpose(2, 1, 0, 3, 4)
        forwarded = forwarded.reshape(N_GRID, N_COMP, N_GRID * OVB, total_comps)
        averaged = lax.map(average_grid, (blocks, forwarded, recv_index, recv_weight))
        spectra = averaged.transpose(0, 2, 1, 3).reshape(N_GRID, total_comps, N_COMP * PTS_DEV)
    return spectra
```

```python
import functools
import math

import jax
import jax.numpy as jnp
import numpy as np
from jax import lax
from jax.experimental import pallas as pl
from jax.experimental.pallas import tpu as pltpu
from jax.sharding import PartitionSpec as P

ND = 36
NF = 32
LX = 128
STEPS = 2


def padded_2(array, sides, width):
    for axis, dim in sides:
        peers, length = (lax.axis_size(axis), array.shape[dim])
        up = [(i, (i + 1) % peers) for i in range(peers - 1)]
        down = [(j, i) for i, j in up]
        last = lax.slice_in_dim(array, length - width, length, axis=dim)
        initial = lax.slice_in_dim(array, 0, width, axis=dim)
        before = lax.ppermute(last, axis, up)
        after = lax.ppermute(initial, axis, down)
        array = jnp.concatenate([before, array, after], axis=dim)
    return array


def courant(comp_index, speed_row):
    direction = comp_index // NF
    frequency = comp_index % NF
    heading = 2.0 * math.pi * direction.astype(jnp.float32) / ND
    onehot_table = (frequency[:, None] == jnp.arange(NF, dtype=jnp.int32)[None, :]).astype(
        jnp.float32
    )
    celerity = jnp.sum(onehot_table * speed_row[None, :], axis=1)
    return (celerity * jnp.cos(heading), celerity * jnp.sin(heading))


def sweep_columns(values, number):
    padded = jnp.pad(values, ((0, 0), (0, 0), (1, 1)))
    forward = padded[:, :, 2:]
    behind = padded[:, :, :-2]
    return (
        values
        - 0.5 * number * (forward - behind)
        + 0.5 * number * number * (forward - 2.0 * values + behind)
    )


def sweep_rows(values, number):
    padded = jnp.pad(values, ((0, 0), (1, 1), (0, 0)))
    forward = padded[:, 2:, :]
    behind = padded[:, :-2, :]
    return (
        values
        - 0.5 * number * (forward - behind)
        + 0.5 * number * number * (forward - 2.0 * values + behind)
    )


def propagate(spectra, sea_float, courant_x, courant_y):
    count = spectra.shape[0]
    values = spectra.astype(jnp.float32).reshape(count, -1, LX)
    land_sea = sea_float.reshape(1, -1, LX)
    values = sweep_columns(values, courant_x[:, None, None]) * land_sea
    values = sweep_rows(values, courant_y[:, None, None]) * land_sea
    return values.reshape(count, -1).astype(jnp.bfloat16)


def advect_block(points, sea_rows, courant_x, courant_y):
    count = points.shape[0]
    values = points.reshape(count, -1, LX)
    extended = padded_2(values, (("comp", 1),), 1)
    widened = extended.astype(jnp.float32)
    widened = sweep_columns(widened, courant_x[:, None, None]) * sea_rows[None]
    widened = sweep_rows(widened, courant_y[:, None, None]) * sea_rows[None]
    return widened[:, 1:-1, :].reshape(count, -1).astype(jnp.bfloat16)


def source(points, sea_part, coupling_a, coupling_b):
    first_term = jnp.dot(coupling_a, points, preferred_element_type=jnp.float32)
    second = jnp.dot(coupling_b, points, preferred_element_type=jnp.float32)
    return (
        points.astype(jnp.float32) + 0.5 * sea_part[None, :] * first_term * jnp.tanh(second)
    ).astype(jnp.bfloat16)


def average(updated, received, targets, weights):
    count = updated.shape[1]
    hits = targets[:, None] == jnp.arange(count, dtype=jnp.int32)[None, :]
    weighted = (received.astype(jnp.float32) * weights[:, None]).astype(jnp.bfloat16)
    onehot_table = hits.astype(jnp.bfloat16)
    gathered_sum = lax.dot_general(
        weighted, onehot_table, (((0,), (0,)), ((), ())), preferred_element_type=jnp.float32
    )
    numerator = updated.astype(jnp.float32) + gathered_sum
    denominator = 1.0 + jnp.sum(hits.astype(jnp.float32) * weights[:, None], axis=0)
    return (numerator / denominator[None, :]).astype(jnp.bfloat16)


def share_intersection(updated, targets, groups, total_comps, my_grid):
    outgoing = jnp.take(updated, targets, axis=1).T.reshape(groups, -1, total_comps)
    everything = lax.all_gather(outgoing, "grid", axis=0, tiled=True)
    received = lax.dynamic_index_in_dim(
        everything.reshape(groups, groups, -1, total_comps), my_grid, 1, keepdims=False
    )
    return received.reshape(-1, total_comps)


def local(spectrum, sea_mask, speed, coupling_a, coupling_b, send_index, recv_index, recv_weight):
    local_comps = spectrum.shape[1]
    columns = spectrum.shape[2]
    groups = lax.axis_size("grid")
    pieces = lax.axis_size("comp")
    block_len = columns // pieces
    total_comps = coupling_a.shape[0]
    comp_index = lax.axis_index("comp") * local_comps + jnp.arange(local_comps, dtype=jnp.int32)
    courant_x, courant_y = courant(comp_index, speed[0])
    sea_float = sea_mask[0].astype(jnp.float32)
    sea_part = lax.dynamic_slice_in_dim(sea_float, lax.axis_index("comp") * block_len, block_len)
    targets = send_index.reshape(-1)
    my_grid = lax.axis_index("grid")
    spectra = spectrum[0]
    full_x, full_y = courant(jnp.arange(total_comps, dtype=jnp.int32), speed[0])
    block_rows = block_len // LX
    padded_sea = jnp.pad(sea_float.reshape(-1, LX), ((1, 1), (0, 0)))
    sea_rows = lax.dynamic_slice_in_dim(
        padded_sea, lax.axis_index("comp") * block_rows, block_rows + 2, 0
    )
    advected = propagate(spectra, sea_float, courant_x, courant_y)
    points = lax.all_to_all(advected, "comp", split_axis=1, concat_axis=0, tiled=True)
    for turn_index in range(STEPS):
        if turn_index > 0:
            points = advect_block(points, sea_rows, full_x, full_y)
        updated = source(points, sea_part, coupling_a, coupling_b)
        received = share_intersection(updated, targets, groups, total_comps, my_grid)
        points = average(updated, received, recv_index[0, 0], recv_weight[0, 0])
    spectra = lax.all_to_all(points, "comp", split_axis=0, concat_axis=1, tiled=True)
    return spectra[None]


MESH = pl.DeviceIdType.MESH
SUB = 16


def coefficients(number):
    square = number * number
    return (1.0 - square, 0.5 * (square - number), 0.5 * (square + number))


def flipped(index, mask, count):
    total = 0
    bit = 1
    while bit < count:
        total = total + lax.rem(index // bit + (mask // bit) % 2, 2) * bit
        bit *= 2
    return total


def wave_kernel(
    sizes,
    spec_ref,
    sea_ref,
    cxy_ref,
    a_hbm,
    b_hbm,
    send_ref,
    recv_ref,
    weight_ref,
    out_ref,
    a_ref,
    b_ref,
    table,
    local_table,
    outbox,
    field,
    updated,
    averaged,
    halo,
    pick_table,
    place_table,
    inverse,
    picked,
    received,
    scaled,
    load_sem,
    first_send,
    first_recv,
    share_send,
    share_recv,
    halo_send,
    halo_recv,
    last_send,
    last_recv,
):
    pieces, groups, own, total, rows, slots = sizes
    block_len = rows * LX
    pairs = rows // 2
    me = lax.axis_index("comp")
    my_grid = lax.axis_index("grid")

    load_a = pltpu.make_async_copy(a_hbm, a_ref, load_sem.at[0])
    load_b = pltpu.make_async_copy(b_hbm, b_ref, load_sem.at[1])
    load_a.start()
    load_b.start()

    barrier = pltpu.get_barrier_semaphore()
    for mask in range(1, pieces):
        pl.semaphore_signal(
            barrier,
            inc=1,
            device_id={"comp": flipped(me, mask, pieces)},
            device_id_type=MESH,
        )
    for shift in range(1, groups):
        pl.semaphore_signal(
            barrier,
            inc=1,
            device_id={"grid": lax.rem(my_grid + shift, groups)},
            device_id_type=MESH,
        )

    lane = lax.broadcasted_iota(jnp.int32, (SUB, LX), 1)

    def fill(source_row, target, target_row):
        cx = jnp.broadcast_to(cxy_ref[pl.ds(source_row, SUB), 0:1], (SUB, LX))
        cy = jnp.broadcast_to(cxy_ref[pl.ds(source_row, SUB), 1:2], (SUB, LX))
        x0, xp, xm = coefficients(cx)
        y0, yp, ym = coefficients(cy)
        here = pl.ds(target_row, SUB)
        target[0, here, :] = x0
        target[1, here, :] = jnp.where(lane == LX - 1, 0.0, xp)
        target[2, here, :] = jnp.where(lane == 0, 0.0, xm)
        target[3, here, :] = y0
        target[4, here, :] = yp
        target[5, here, :] = ym

    def fill_local(step, carry):
        fill(
            pl.multiple_of(me * own + step * SUB, SUB),
            local_table,
            pl.multiple_of(step * SUB, SUB),
        )
        return carry

    lax.fori_loop(0, own // SUB, fill_local, 0)

    def swept(value, sea, coefs):
        return (
            coefs[0] * value
            + coefs[1] * pltpu.roll(value, LX - 1, 1)
            + coefs[2] * pltpu.roll(value, 1, 1)
        ) * sea

    def crossed(middle, above, below, sea, coefs):
        return ((coefs[3] * middle + coefs[4] * above + coefs[5] * below) * sea).astype(
            jnp.bfloat16
        )

    lattice_rows = pieces * rows

    def advect_first(peer, pair, store):
        base = peer * rows + 2 * pair
        where_rows = [
            jnp.minimum(jnp.maximum(base - 1 + t, 0), lattice_rows - 1) for t in range(4)
        ]
        seas = [sea_ref[base + t] for t in range(4)]

        def step(block, carry):
            here = pl.ds(pl.multiple_of(block * SUB, SUB), SUB)
            coefs = [local_table[i, here, :] for i in range(6)]
            lines = [
                swept(
                    spec_ref[here, pl.ds(pl.multiple_of(row * LX, LX), LX)].astype(jnp.float32),
                    seas[t],
                    coefs,
                )
                for t, row in enumerate(where_rows)
            ]
            for t in range(2):
                store(t, block, crossed(lines[t + 1], lines[t + 2], lines[t], seas[t + 1], coefs))
            return carry

        lax.fori_loop(0, own // SUB, step, 0)

    order = list(range(pieces - 1, 0, -1))
    mine = pl.ds(pl.multiple_of(me * own, SUB), own)

    def first_copy(pair, mask):
        return pltpu.make_async_remote_copy(
            src_ref=outbox.at[pair, mask],
            dst_ref=field.at[pl.ds(2 * pair, 2), mine, :],
            send_sem=first_send.at[pair, mask],
            recv_sem=first_recv.at[pair, mask],
            device_id={"comp": flipped(me, mask, pieces)},
            device_id_type=MESH,
        )

    for pair in range(pairs):
        for mask in order:

            def store_out(t, block, value, pair=pair, mask=mask):
                here = pl.ds(pl.multiple_of(block * SUB, SUB), SUB)
                outbox[pair, mask, t, here, :] = value

            advect_first(flipped(me, mask, pieces), pair, store_out)
            if pair == 0 and mask == order[0]:
                pl.semaphore_wait(barrier, pieces - 1 + groups - 1)
            first_copy(pair, mask).start()

    for pair in range(pairs):

        def store_own(t, block, value, pair=pair):
            here = pl.ds(pl.multiple_of(me * own + block * SUB, SUB), SUB)
            field[2 * pair + t, here, :] = value

        advect_first(me, pair, store_own)

    def fill_all(step, carry):
        row = pl.multiple_of(step * SUB, SUB)
        fill(row, table, row)
        return carry

    lax.fori_loop(0, total // SUB, fill_all, 0)

    places = groups * slots
    point = lax.broadcasted_iota(jnp.int32, (places, block_len), 1)
    pick_table[...] = (send_ref[...] == point).astype(jnp.float32).astype(jnp.bfloat16)
    hits = (recv_ref[...] == point).astype(jnp.float32)
    place_table[...] = hits.astype(jnp.bfloat16)
    inverse[...] = 1.0 / (1.0 + jnp.sum(hits * weight_ref[...], axis=0, keepdims=True))

    @pl.when(me == 0)
    def _():
        halo[0] = jnp.zeros_like(halo[0])

    @pl.when(me == pieces - 1)
    def _():
        halo[1] = jnp.zeros_like(halo[1])

    load_a.wait()
    load_b.wait()

    tall = total // 3 if total % (3 * SUB) == 0 else total

    def source_rows(one, two):
        half = 0.5 * jnp.concatenate(
            [sea_ref[me * rows + 1 + one], sea_ref[me * rows + 1 + two]], axis=1
        )

        def step(index, carry):
            here = pl.ds(pl.multiple_of(index * tall, SUB), tall)
            values = jnp.concatenate([field[one], field[two]], axis=1)
            first = jnp.dot(a_ref[here, :], values, preferred_element_type=jnp.float32)
            second = jnp.dot(b_ref[here, :], values, preferred_element_type=jnp.float32)
            own_values = jnp.concatenate([field[one, here, :], field[two, here, :]], axis=1)
            result = (own_values.astype(jnp.float32) + half * first * jnp.tanh(second)).astype(
                jnp.bfloat16
            )
            updated[one, here, :] = result[:, :LX]
            updated[two, here, :] = result[:, LX:]
            return carry

        lax.fori_loop(0, total // tall, step, 0)

    def share_copy(turn, shift):
        peer = lax.rem(my_grid + shift, groups)
        return pltpu.make_async_remote_copy(
            src_ref=picked.at[pl.ds(pl.multiple_of(peer * slots, SUB), slots), :],
            dst_ref=received.at[turn, pl.ds(pl.multiple_of(my_grid * slots, SUB), slots), :],
            send_sem=share_send.at[turn, shift],
            recv_sem=share_recv.at[turn, shift],
            device_id={"grid": peer},
            device_id_type=MESH,
        )

    def share(turn):
        everything = jnp.concatenate([updated[r] for r in range(rows)], axis=1)
        chosen = lax.dot_general(
            pick_table[...],
            everything,
            (((1,), (1,)), ((), ())),
            preferred_element_type=jnp.float32,
        )
        picked[...] = chosen.astype(jnp.bfloat16)
        for shift in range(1, groups):
            share_copy(turn, shift).start()
        here = pl.ds(pl.multiple_of(my_grid * slots, SUB), slots)
        received[turn, here, :] = picked[here, :]
        for shift in range(1, groups):
            share_copy(turn, shift).wait()
        scaled[...] = (
            (received[turn].astype(jnp.float32) * weight_ref[...])
            .astype(jnp.bfloat16)
            .astype(jnp.float32)
            .T.astype(jnp.bfloat16)
        )

    def average_rows(here, wanted):
        for row in wanted:
            columns = slice(row * LX, (row + 1) * LX)
            added = jnp.dot(
                scaled[here, :], place_table[:, columns], preferred_element_type=jnp.float32
            )
            averaged[row, here, :] = (
                (updated[row, here, :].astype(jnp.float32) + added) * inverse[:, columns]
            ).astype(jnp.bfloat16)

    def halo_up():
        return pltpu.make_async_remote_copy(
            src_ref=averaged.at[rows - 1],
            dst_ref=halo.at[0],
            send_sem=halo_send.at[0],
            recv_sem=halo_recv.at[0],
            device_id={"comp": jnp.minimum(me + 1, pieces - 1)},
            device_id_type=MESH,
        )

    def halo_down():
        return pltpu.make_async_remote_copy(
            src_ref=averaged.at[0],
            dst_ref=halo.at[1],
            send_sem=halo_send.at[1],
            recv_sem=halo_recv.at[1],
            device_id={"comp": jnp.maximum(me - 1, 0)},
            device_id_type=MESH,
        )

    def advect_rows(wanted):
        def step(block, carry):
            here = pl.ds(pl.multiple_of(block * SUB, SUB), SUB)
            coefs = [table[i, here, :] for i in range(6)]
            lines = {}

            def line(row):
                if row not in lines:
                    if row < 0:
                        raw = halo[0, here, :]
                    elif row >= rows:
                        raw = halo[1, here, :]
                    else:
                        raw = averaged[row, here, :]
                    lines[row] = swept(
                        raw.astype(jnp.float32), sea_ref[me * rows + 1 + row], coefs
                    )
                return lines[row]

            for row in wanted:
                field[row, here, :] = crossed(
                    line(row), line(row + 1), line(row - 1), sea_ref[me * rows + 1 + row], coefs
                )
            return carry

        lax.fori_loop(0, total // SUB, step, 0)

    for pair in range(pairs):
        for mask in order:
            first_copy(pair, mask).wait_recv()
        source_rows(2 * pair, 2 * pair + 1)
    for pair in range(pairs):
        for mask in order:
            first_copy(pair, mask).wait_send()

    inner = list(range(1, rows - 1))
    whole = pl.ds(0, total)
    for turn in range(STEPS):
        if turn > 0:

            def average_step(index, carry, wanted):
                average_rows(pl.ds(pl.multiple_of(index * own, SUB), own), wanted)
                return carry

            lax.fori_loop(
                0, total // own, functools.partial(average_step, wanted=(0, rows - 1)), 0
            )

            @pl.when(me < pieces - 1)
            def _():
                halo_up().start()

            @pl.when(me > 0)
            def _():
                halo_down().start()

            lax.fori_loop(0, total // own, functools.partial(average_step, wanted=inner), 0)
            advect_rows(inner)
            for pair in range(len(inner) // 2):
                source_rows(inner[2 * pair], inner[2 * pair + 1])

            @pl.when(me < pieces - 1)
            def _():
                halo_up().wait_send()
                halo_down().wait_recv()

            @pl.when(me > 0)
            def _():
                halo_down().wait_send()
                halo_up().wait_recv()

            advect_rows((0, rows - 1))
            source_rows(0, rows - 1)
        share(turn)

    def last_copy(mask):
        peer = flipped(me, mask, pieces)
        return pltpu.make_async_remote_copy(
            src_ref=averaged.at[:, pl.ds(pl.multiple_of(peer * own, SUB), own), :],
            dst_ref=out_ref.at[pl.ds(me * rows, rows)],
            send_sem=last_send.at[mask],
            recv_sem=last_recv.at[mask],
            device_id={"comp": peer},
            device_id_type=MESH,
        )

    for mask in order:
        peer = flipped(me, mask, pieces)
        average_rows(pl.ds(pl.multiple_of(peer * own, SUB), own), range(rows))
        last_copy(mask).start()
    average_rows(mine, range(rows))
    for row in range(rows):
        out_ref[me * rows + row] = averaged[row, mine, :]
    for mask in order:
        last_copy(mask).wait()


def fused(spectrum, sea_mask, speed, coupling_a, coupling_b, send_index, recv_index, recv_weight):
    own, columns = spectrum.shape[1:]
    pieces = lax.axis_size("comp")
    groups = lax.axis_size("grid")
    total = coupling_a.shape[0]
    rows = columns // pieces // LX
    slots = send_index.shape[-1]
    places = groups * slots
    heading = (2.0 * math.pi / ND) * (np.arange(total) // NF)
    turns = np.stack([np.cos(heading), np.sin(heading)], axis=1).astype(np.float32)
    cxy = jnp.tile(speed[0], total // NF)[:, None] * jnp.asarray(turns)
    sea = jnp.pad(sea_mask[0].astype(jnp.float32).reshape(-1, 1, LX), ((1, 1), (0, 0), (0, 0)))
    vmem = pl.BlockSpec(memory_space=pltpu.VMEM)
    anywhere = pl.BlockSpec(memory_space=pl.ANY)
    half = jnp.bfloat16
    dma = pltpu.SemaphoreType.DMA
    lines = pl.pallas_call(
        functools.partial(wave_kernel, (pieces, groups, own, total, rows, slots)),
        out_shape=jax.ShapeDtypeStruct((pieces * rows, own, LX), half),
        in_specs=[vmem, vmem, vmem, anywhere, anywhere, vmem, vmem, vmem],
        out_specs=vmem,
        scratch_shapes=[
            pltpu.VMEM(coupling_a.shape, half),
            pltpu.VMEM(coupling_b.shape, half),
            pltpu.VMEM((6, total, LX), jnp.float32),
            pltpu.VMEM((6, own, LX), jnp.float32),
            pltpu.VMEM((rows // 2, pieces, 2, own, LX), half),
            pltpu.VMEM((rows, total, LX), half),
            pltpu.VMEM((rows, total, LX), half),
            pltpu.VMEM((rows, total, LX), half),
            pltpu.VMEM((2, total, LX), half),
            pltpu.VMEM((places, rows * LX), half),
            pltpu.VMEM((places, rows * LX), half),
            pltpu.VMEM((1, rows * LX), jnp.float32),
            pltpu.VMEM((places, total), half),
            pltpu.VMEM((STEPS, places, total), half),
            pltpu.VMEM((total, places), half),
            dma((2,)),
            dma((rows // 2, pieces)),
            dma((rows // 2, pieces)),
            dma((STEPS, groups)),
            dma((STEPS, groups)),
            dma((2,)),
            dma((2,)),
            dma((pieces,)),
            dma((pieces,)),
        ],
        compiler_params=pltpu.CompilerParams(
            collective_id=0, has_side_effects=True, vmem_limit_bytes=48 * 1024 * 1024
        ),
        name="wave_steps",
    )(
        spectrum[0],
        sea,
        cxy,
        coupling_a,
        coupling_b,
        send_index.reshape(places, 1),
        recv_index.reshape(places, 1),
        recv_weight.reshape(places, 1),
    )
    return lines.transpose(1, 0, 2).reshape(1, own, columns)


def fits(pieces, groups, own, rows, slots):
    power = pieces & (pieces - 1) == 0
    return power and own % SUB == 0 and rows % 2 == 0 and rows >= 4 and slots % SUB == 0


def program(spectrum, sea_mask, speed, coupling_a, coupling_b, send_index, recv_index, recv_weight):
    pieces = lax.axis_size("comp")
    groups = lax.axis_size("grid")
    rows = spectrum.shape[2] // pieces // LX
    whole = rows * pieces * LX == spectrum.shape[2]
    chosen = local
    if whole and fits(pieces, groups, spectrum.shape[1], rows, send_index.shape[-1]):
        chosen = fused
    return chosen(
        spectrum, sea_mask, speed, coupling_a, coupling_b, send_index, recv_index, recv_weight
    )


def solution(mesh):
    return jax.shard_map(
        program,
        mesh=mesh,
        in_specs=(
            P("grid", "comp", None),
            P("grid", None),
            P("grid", None),
            P(),
            P(),
            P("grid", "comp", None, None),
            P("grid", "comp", None),
            P("grid", "comp", None),
        ),
        out_specs=P("grid", "comp", None),
        check_vma=False,
    )
```

```python
import functools
import math

import jax
import jax.numpy as jnp
import numpy as np
from jax import lax
from jax.experimental import pallas as pl
from jax.experimental.pallas import tpu as pltpu
from jax.sharding import PartitionSpec as P

ND = 36
NF = 32
LX = 128
STEPS = 2


def padded_2(array, sides, width):
    for axis, dim in sides:
        peers, length = (lax.axis_size(axis), array.shape[dim])
        up = [(i, (i + 1) % peers) for i in range(peers - 1)]
        down = [(j, i) for i, j in up]
        last = lax.slice_in_dim(array, length - width, length, axis=dim)
        initial = lax.slice_in_dim(array, 0, width, axis=dim)
        before = lax.ppermute(last, axis, up)
        after = lax.ppermute(initial, axis, down)
        array = jnp.concatenate([before, array, after], axis=dim)
    return array


def courant(comp_index, speed_row):
    direction = comp_index // NF
    frequency = comp_index % NF
    heading = 2.0 * math.pi * direction.astype(jnp.float32) / ND
    onehot_table = (frequency[:, None] == jnp.arange(NF, dtype=jnp.int32)[None, :]).astype(
        jnp.float32
    )
    celerity = jnp.sum(onehot_table * speed_row[None, :], axis=1)
    return (celerity * jnp.cos(heading), celerity * jnp.sin(heading))


def sweep_columns(values, number):
    padded = jnp.pad(values, ((0, 0), (0, 0), (1, 1)))
    forward = padded[:, :, 2:]
    behind = padded[:, :, :-2]
    return (
        values
        - 0.5 * number * (forward - behind)
        + 0.5 * number * number * (forward - 2.0 * values + behind)
    )


def sweep_rows(values, number):
    padded = jnp.pad(values, ((0, 0), (1, 1), (0, 0)))
    forward = padded[:, 2:, :]
    behind = padded[:, :-2, :]
    return (
        values
        - 0.5 * number * (forward - behind)
        + 0.5 * number * number * (forward - 2.0 * values + behind)
    )


def propagate(spectra, sea_float, courant_x, courant_y):
    count = spectra.shape[0]
    values = spectra.astype(jnp.float32).reshape(count, -1, LX)
    land_sea = sea_float.reshape(1, -1, LX)
    values = sweep_columns(values, courant_x[:, None, None]) * land_sea
    values = sweep_rows(values, courant_y[:, None, None]) * land_sea
    return values.reshape(count, -1).astype(jnp.bfloat16)


def advect_block(points, sea_rows, courant_x, courant_y):
    count = points.shape[0]
    values = points.reshape(count, -1, LX)
    extended = padded_2(values, (("comp", 1),), 1)
    widened = extended.astype(jnp.float32)
    widened = sweep_columns(widened, courant_x[:, None, None]) * sea_rows[None]
    widened = sweep_rows(widened, courant_y[:, None, None]) * sea_rows[None]
    return widened[:, 1:-1, :].reshape(count, -1).astype(jnp.bfloat16)


def source(points, sea_part, coupling_a, coupling_b):
    first_term = jnp.dot(coupling_a, points, preferred_element_type=jnp.float32)
    second = jnp.dot(coupling_b, points, preferred_element_type=jnp.float32)
    return (
        points.astype(jnp.float32) + 0.5 * sea_part[None, :] * first_term * jnp.tanh(second)
    ).astype(jnp.bfloat16)


def average(updated, received, targets, weights):
    count = updated.shape[1]
    hits = targets[:, None] == jnp.arange(count, dtype=jnp.int32)[None, :]
    weighted = (received.astype(jnp.float32) * weights[:, None]).astype(jnp.bfloat16)
    onehot_table = hits.astype(jnp.bfloat16)
    gathered_sum = lax.dot_general(
        weighted, onehot_table, (((0,), (0,)), ((), ())), preferred_element_type=jnp.float32
    )
    numerator = updated.astype(jnp.float32) + gathered_sum
    denominator = 1.0 + jnp.sum(hits.astype(jnp.float32) * weights[:, None], axis=0)
    return (numerator / denominator[None, :]).astype(jnp.bfloat16)


def share_intersection(updated, targets, groups, total_comps, my_grid):
    outgoing = jnp.take(updated, targets, axis=1).T.reshape(groups, -1, total_comps)
    everything = lax.all_gather(outgoing, "grid", axis=0, tiled=True)
    received = lax.dynamic_index_in_dim(
        everything.reshape(groups, groups, -1, total_comps), my_grid, 1, keepdims=False
    )
    return received.reshape(-1, total_comps)


def local(spectrum, sea_mask, speed, coupling_a, coupling_b, send_index, recv_index, recv_weight):
    local_comps = spectrum.shape[1]
    columns = spectrum.shape[2]
    groups = lax.axis_size("grid")
    pieces = lax.axis_size("comp")
    block_len = columns // pieces
    total_comps = coupling_a.shape[0]
    comp_index = lax.axis_index("comp") * local_comps + jnp.arange(local_comps, dtype=jnp.int32)
    courant_x, courant_y = courant(comp_index, speed[0])
    sea_float = sea_mask[0].astype(jnp.float32)
    sea_part = lax.dynamic_slice_in_dim(sea_float, lax.axis_index("comp") * block_len, block_len)
    targets = send_index.reshape(-1)
    my_grid = lax.axis_index("grid")
    spectra = spectrum[0]
    full_x, full_y = courant(jnp.arange(total_comps, dtype=jnp.int32), speed[0])
    block_rows = block_len // LX
    padded_sea = jnp.pad(sea_float.reshape(-1, LX), ((1, 1), (0, 0)))
    sea_rows = lax.dynamic_slice_in_dim(
        padded_sea, lax.axis_index("comp") * block_rows, block_rows + 2, 0
    )
    advected = propagate(spectra, sea_float, courant_x, courant_y)
    points = lax.all_to_all(advected, "comp", split_axis=1, concat_axis=0, tiled=True)
    for turn_index in range(STEPS):
        if turn_index > 0:
            points = advect_block(points, sea_rows, full_x, full_y)
        updated = source(points, sea_part, coupling_a, coupling_b)
        received = share_intersection(updated, targets, groups, total_comps, my_grid)
        points = average(updated, received, recv_index[0, 0], recv_weight[0, 0])
    spectra = lax.all_to_all(points, "comp", split_axis=0, concat_axis=1, tiled=True)
    return spectra[None]


MESH = pl.DeviceIdType.MESH
SUB = 16


def coefficients(number):
    square = number * number
    return (1.0 - square, 0.5 * (square - number), 0.5 * (square + number))


def flipped(index, mask, count):
    total = 0
    bit = 1
    while bit < count:
        total = total + lax.rem(index // bit + (mask // bit) % 2, 2) * bit
        bit *= 2
    return total


def wave_kernel(
    sizes,
    spec_hbm,
    sea_ref,
    speed_ref,
    turn_ref,
    a_hbm,
    b_hbm,
    send_ref,
    recv_ref,
    weight_ref,
    out_ref,
    spec_ref,
    celerity,
    a_ref,
    b_ref,
    table,
    local_table,
    outbox,
    field,
    updated,
    averaged,
    final,
    halo,
    pick_table,
    place_table,
    inverse,
    weight,
    picked,
    received,
    scaled,
    load_sem,
    first_send,
    first_recv,
    share_send,
    share_recv,
    halo_send,
    halo_recv,
    last_send,
    last_recv,
):
    pieces, groups, own, total, rows, slots = sizes
    block_len = rows * LX
    pairs = rows // 2
    me = lax.axis_index("comp")
    my_grid = lax.axis_index("grid")

    load_a = pltpu.make_async_copy(a_hbm, a_ref, load_sem.at[0])
    load_b = pltpu.make_async_copy(b_hbm, b_ref, load_sem.at[1])
    load_spec = pltpu.make_async_copy(spec_hbm, spec_ref, load_sem.at[2])
    load_spec.start()

    barrier = pltpu.get_barrier_semaphore()
    for mask in range(1, pieces):
        pl.semaphore_signal(
            barrier,
            inc=1,
            device_id={"comp": flipped(me, mask, pieces)},
            device_id_type=MESH,
        )
    for shift in range(1, groups):
        pl.semaphore_signal(
            barrier,
            inc=1,
            device_id={"grid": lax.rem(my_grid + shift, groups)},
            device_id_type=MESH,
        )

    lane = lax.broadcasted_iota(jnp.int32, (SUB, LX), 1)

    def upright(row):
        length = row.shape[1]
        across = lax.broadcasted_iota(jnp.int32, (length, length), 1)
        down = lax.broadcasted_iota(jnp.int32, (length, length), 0)
        square = jnp.broadcast_to(row.astype(jnp.float32), (length, length))
        return jnp.sum(jnp.where(across == down, square, 0.0), axis=1, keepdims=True)

    celerity[...] = jnp.broadcast_to(upright(speed_ref[...]), celerity.shape)

    def fill(source_row, target, target_row):
        part = pl.multiple_of(lax.rem(source_row, NF), SUB)
        pace = celerity[pl.ds(part, SUB), :]
        cx = pace * turn_ref[0, source_row // NF]
        cy = pace * turn_ref[1, source_row // NF]
        x0, xp, xm = coefficients(cx)
        y0, yp, ym = coefficients(cy)
        here = pl.ds(target_row, SUB)
        target[0, here, :] = x0
        target[1, here, :] = jnp.where(lane == LX - 1, 0.0, xp)
        target[2, here, :] = jnp.where(lane == 0, 0.0, xm)
        target[3, here, :] = y0
        target[4, here, :] = yp
        target[5, here, :] = ym

    def fill_local(step, carry):
        fill(
            pl.multiple_of(me * own + step * SUB, SUB),
            local_table,
            pl.multiple_of(step * SUB, SUB),
        )
        return carry

    lax.fori_loop(0, own // SUB, fill_local, 0)

    def swept(value, sea, coefs):
        return (
            coefs[0] * value
            + coefs[1] * pltpu.roll(value, LX - 1, 1)
            + coefs[2] * pltpu.roll(value, 1, 1)
        ) * sea

    def crossed(middle, above, below, sea, coefs):
        return ((coefs[3] * middle + coefs[4] * above + coefs[5] * below) * sea).astype(
            jnp.bfloat16
        )

    lattice_rows = pieces * rows
    load_spec.wait()
    load_a.start()
    load_b.start()

    def sea_line(row):
        inside = jnp.minimum(jnp.maximum(row, 0), lattice_rows - 1)
        line = sea_ref[:, pl.ds(pl.multiple_of(inside * LX, LX), LX)]
        return jnp.where(inside == row, line, 0).astype(jnp.float32)

    def advect_first(peer, pair, store):
        base = peer * rows + 2 * pair
        where_rows = [
            jnp.minimum(jnp.maximum(base - 1 + t, 0), lattice_rows - 1) for t in range(4)
        ]
        seas = [sea_line(base - 1 + t) for t in range(4)]

        def step(block, carry):
            here = pl.ds(pl.multiple_of(block * SUB, SUB), SUB)
            coefs = [local_table[i, here, :] for i in range(6)]
            lines = [
                swept(
                    spec_ref[here, pl.ds(pl.multiple_of(row * LX, LX), LX)].astype(jnp.float32),
                    seas[t],
                    coefs,
                )
                for t, row in enumerate(where_rows)
            ]
            for t in range(2):
                store(t, block, crossed(lines[t + 1], lines[t + 2], lines[t], seas[t + 1], coefs))
            return carry

        lax.fori_loop(0, own // SUB, step, 0)

    order = list(range(pieces - 1, 0, -1))
    mine = pl.ds(pl.multiple_of(me * own, SUB), own)

    def first_copy(pair, mask):
        return pltpu.make_async_remote_copy(
            src_ref=outbox.at[pair, mask],
            dst_ref=field.at[pl.ds(2 * pair, 2), mine, :],
            send_sem=first_send.at[pair, mask],
            recv_sem=first_recv.at[pair, mask],
            device_id={"comp": flipped(me, mask, pieces)},
            device_id_type=MESH,
        )

    for pair in range(pairs):
        for mask in order:

            def store_out(t, block, value, pair=pair, mask=mask):
                here = pl.ds(pl.multiple_of(block * SUB, SUB), SUB)
                outbox[pair, mask, t, here, :] = value

            advect_first(flipped(me, mask, pieces), pair, store_out)
            if pair == 0 and mask == order[0]:
                pl.semaphore_wait(barrier, pieces - 1 + groups - 1)
            first_copy(pair, mask).start()

    for pair in range(pairs):

        def store_own(t, block, value, pair=pair):
            here = pl.ds(pl.multiple_of(me * own + block * SUB, SUB), SUB)
            field[2 * pair + t, here, :] = value

        advect_first(me, pair, store_own)

    def fill_all(step, carry):
        row = pl.multiple_of(step * SUB, SUB)
        fill(row, table, row)
        return carry

    lax.fori_loop(0, total // SUB, fill_all, 0)

    places = groups * slots
    point = lax.broadcasted_iota(jnp.int32, (places, block_len), 1)
    spot = lax.broadcasted_iota(jnp.int32, (slots, block_len), 1).astype(jnp.float32)
    for group in range(groups):
        wanted = upright(send_ref[group : group + 1, :]) == spot
        pick_table[group * slots : (group + 1) * slots, :] = wanted.astype(jnp.float32).astype(
            jnp.bfloat16
        )
    hits = (upright(recv_ref[...]) == point.astype(jnp.float32)).astype(jnp.float32)
    place_table[...] = hits.astype(jnp.bfloat16)
    weight[...] = upright(weight_ref[...])
    inverse[...] = 1.0 / (1.0 + jnp.sum(hits * weight[...], axis=0, keepdims=True))

    @pl.when(me == 0)
    def _():
        halo[0] = jnp.zeros_like(halo[0])

    @pl.when(me == pieces - 1)
    def _():
        halo[1] = jnp.zeros_like(halo[1])

    load_a.wait()
    load_b.wait()

    tall = total // 3 if total % (3 * SUB) == 0 else total

    def source_rows(one, two):
        half = 0.5 * jnp.concatenate(
            [sea_line(me * rows + one), sea_line(me * rows + two)], axis=1
        )

        def step(index, carry):
            here = pl.ds(pl.multiple_of(index * tall, SUB), tall)
            values = jnp.concatenate([field[one], field[two]], axis=1)
            first = jnp.dot(a_ref[here, :], values, preferred_element_type=jnp.float32)
            second = jnp.dot(b_ref[here, :], values, preferred_element_type=jnp.float32)
            own_values = jnp.concatenate([field[one, here, :], field[two, here, :]], axis=1)
            result = (own_values.astype(jnp.float32) + half * first * jnp.tanh(second)).astype(
                jnp.bfloat16
            )
            updated[one, here, :] = result[:, :LX]
            updated[two, here, :] = result[:, LX:]
            return carry

        lax.fori_loop(0, total // tall, step, 0)

    def share_copy(turn, shift):
        peer = lax.rem(my_grid + shift, groups)
        return pltpu.make_async_remote_copy(
            src_ref=picked.at[pl.ds(pl.multiple_of(peer * slots, SUB), slots), :],
            dst_ref=received.at[turn, pl.ds(pl.multiple_of(my_grid * slots, SUB), slots), :],
            send_sem=share_send.at[turn, shift],
            recv_sem=share_recv.at[turn, shift],
            device_id={"grid": peer},
            device_id_type=MESH,
        )

    def share(turn):
        everything = jnp.concatenate([updated[r] for r in range(rows)], axis=1)
        chosen = lax.dot_general(
            pick_table[...],
            everything,
            (((1,), (1,)), ((), ())),
            preferred_element_type=jnp.float32,
        )
        picked[...] = chosen.astype(jnp.bfloat16)
        for shift in range(1, groups):
            share_copy(turn, shift).start()
        here = pl.ds(pl.multiple_of(my_grid * slots, SUB), slots)
        received[turn, here, :] = picked[here, :]
        for shift in range(1, groups):
            share_copy(turn, shift).wait()
        scaled[...] = (
            (received[turn].astype(jnp.float32) * weight[...])
            .astype(jnp.bfloat16)
            .astype(jnp.float32)
            .T.astype(jnp.bfloat16)
        )

    def average_rows(here, wanted, store):
        for row in wanted:
            columns = slice(row * LX, (row + 1) * LX)
            added = jnp.dot(
                scaled[here, :], place_table[:, columns], preferred_element_type=jnp.float32
            )
            value = (updated[row, here, :].astype(jnp.float32) + added) * inverse[:, columns]
            store(row, value.astype(jnp.bfloat16))

    def halo_up():
        return pltpu.make_async_remote_copy(
            src_ref=averaged.at[rows - 1],
            dst_ref=halo.at[0],
            send_sem=halo_send.at[0],
            recv_sem=halo_recv.at[0],
            device_id={"comp": jnp.minimum(me + 1, pieces - 1)},
            device_id_type=MESH,
        )

    def halo_down():
        return pltpu.make_async_remote_copy(
            src_ref=averaged.at[0],
            dst_ref=halo.at[1],
            send_sem=halo_send.at[1],
            recv_sem=halo_recv.at[1],
            device_id={"comp": jnp.maximum(me - 1, 0)},
            device_id_type=MESH,
        )

    def advect_rows(wanted):
        seas = {row: sea_line(me * rows + row) for row in range(-1, rows + 1)}

        def step(block, carry):
            here = pl.ds(pl.multiple_of(block * SUB, SUB), SUB)
            coefs = [table[i, here, :] for i in range(6)]
            lines = {}

            def line(row):
                if row not in lines:
                    if row < 0:
                        raw = halo[0, here, :]
                    elif row >= rows:
                        raw = halo[1, here, :]
                    else:
                        raw = averaged[row, here, :]
                    lines[row] = swept(raw.astype(jnp.float32), seas[row], coefs)
                return lines[row]

            for row in wanted:
                field[row, here, :] = crossed(
                    line(row), line(row + 1), line(row - 1), seas[row], coefs
                )
            return carry

        lax.fori_loop(0, total // SUB, step, 0)

    for pair in range(pairs):
        for mask in order:
            first_copy(pair, mask).wait_recv()
        source_rows(2 * pair, 2 * pair + 1)
    for pair in range(pairs):
        for mask in order:
            first_copy(pair, mask).wait_send()

    inner = list(range(1, rows - 1))
    whole = pl.ds(0, total)
    for turn in range(STEPS):
        if turn > 0:

            def average_step(index, carry, wanted):
                here = pl.ds(pl.multiple_of(index * own, SUB), own)

                def store_row(row, value):
                    averaged[row, here, :] = value

                average_rows(here, wanted, store_row)
                return carry

            lax.fori_loop(
                0, total // own, functools.partial(average_step, wanted=(0, rows - 1)), 0
            )

            @pl.when(me < pieces - 1)
            def _():
                halo_up().start()

            @pl.when(me > 0)
            def _():
                halo_down().start()

            lax.fori_loop(0, total // own, functools.partial(average_step, wanted=inner), 0)
            advect_rows(inner)
            for pair in range(len(inner) // 2):
                source_rows(inner[2 * pair], inner[2 * pair + 1])

            @pl.when(me < pieces - 1)
            def _():
                halo_up().wait_send()
                halo_down().wait_recv()

            @pl.when(me > 0)
            def _():
                halo_down().wait_send()
                halo_up().wait_recv()

            advect_rows((0, rows - 1))
            source_rows(0, rows - 1)
        share(turn)

    def block_rows(peer):
        return pl.ds(pl.multiple_of(peer * own, SUB), own)

    my_points = pl.multiple_of(me * block_len, LX)

    def last_copy(mask):
        peer = flipped(me, mask, pieces)
        return pltpu.make_async_remote_copy(
            src_ref=final.at[block_rows(peer), :],
            dst_ref=out_ref.at[:, pl.ds(my_points, block_len)],
            send_sem=last_send.at[mask],
            recv_sem=last_recv.at[mask],
            device_id={"comp": peer},
            device_id_type=MESH,
        )

    for mask in order:
        here = block_rows(flipped(me, mask, pieces))

        def store_final(row, value, here=here):
            final[here, row * LX : (row + 1) * LX] = value

        average_rows(here, range(rows), store_final)
        last_copy(mask).start()

    def store_mine(row, value):
        out_ref[:, pl.ds(pl.multiple_of(my_points + row * LX, LX), LX)] = value

    average_rows(mine, range(rows), store_mine)
    for mask in order:
        last_copy(mask).wait()


def fused(spectrum, sea_mask, speed, coupling_a, coupling_b, send_index, recv_index, recv_weight):
    own, columns = spectrum.shape[1:]
    pieces = lax.axis_size("comp")
    groups = lax.axis_size("grid")
    total = coupling_a.shape[0]
    rows = columns // pieces // LX
    slots = send_index.shape[-1]
    places = groups * slots
    heading = (2.0 * math.pi / ND) * np.arange(total // NF)
    turns = np.stack([np.cos(heading), np.sin(heading)]).astype(np.float32)
    vmem = pl.BlockSpec(memory_space=pltpu.VMEM)
    anywhere = pl.BlockSpec(memory_space=pltpu.HBM)
    half = jnp.bfloat16
    dma = pltpu.SemaphoreType.DMA
    smem = pl.BlockSpec(memory_space=pltpu.SMEM)
    lines = pl.pallas_call(
        functools.partial(wave_kernel, (pieces, groups, own, total, rows, slots)),
        out_shape=jax.ShapeDtypeStruct((own, columns), half),
        in_specs=[anywhere, vmem, vmem, smem, anywhere, anywhere, vmem, vmem, vmem],
        out_specs=vmem,
        scratch_shapes=[
            pltpu.VMEM((own, columns), half),
            pltpu.VMEM((NF, LX), jnp.float32),
            pltpu.VMEM(coupling_a.shape, half),
            pltpu.VMEM(coupling_b.shape, half),
            pltpu.VMEM((6, total, LX), jnp.float32),
            pltpu.VMEM((6, own, LX), jnp.float32),
            pltpu.VMEM((rows // 2, pieces, 2, own, LX), half),
            pltpu.VMEM((rows, total, LX), half),
            pltpu.VMEM((rows, total, LX), half),
            pltpu.VMEM((rows, total, LX), half),
            pltpu.VMEM((total, rows * LX), half),
            pltpu.VMEM((2, total, LX), half),
            pltpu.VMEM((places, rows * LX), half),
            pltpu.VMEM((places, rows * LX), half),
            pltpu.VMEM((1, rows * LX), jnp.float32),
            pltpu.VMEM((places, 1), jnp.float32),
            pltpu.VMEM((places, total), half),
            pltpu.VMEM((STEPS, places, total), half),
            pltpu.VMEM((total, places), half),
            dma((3,)),
            dma((rows // 2, pieces)),
            dma((rows // 2, pieces)),
            dma((STEPS, groups)),
            dma((STEPS, groups)),
            dma((2,)),
            dma((2,)),
            dma((pieces,)),
            dma((pieces,)),
        ],
        compiler_params=pltpu.CompilerParams(
            collective_id=0, has_side_effects=True, vmem_limit_bytes=64900000
        ),
        name="wave_steps",
    )(
        spectrum[0],
        sea_mask,
        speed,
        jnp.asarray(turns),
        coupling_a,
        coupling_b,
        send_index[0, 0],
        recv_index[0],
        recv_weight[0],
    )
    return lines[None]


def fits(pieces, groups, own, rows, slots):
    power = pieces & (pieces - 1) == 0
    return power and own % SUB == 0 and rows % 2 == 0 and rows >= 4 and slots % SUB == 0


def program(spectrum, sea_mask, speed, coupling_a, coupling_b, send_index, recv_index, recv_weight):
    pieces = lax.axis_size("comp")
    groups = lax.axis_size("grid")
    rows = spectrum.shape[2] // pieces // LX
    whole = rows * pieces * LX == spectrum.shape[2]
    chosen = local
    if whole and fits(pieces, groups, spectrum.shape[1], rows, send_index.shape[-1]):
        chosen = fused
    return chosen(
        spectrum, sea_mask, speed, coupling_a, coupling_b, send_index, recv_index, recv_weight
    )


def solution(mesh):
    return jax.shard_map(
        program,
        mesh=mesh,
        in_specs=(
            P("grid", "comp", None),
            P("grid", None),
            P("grid", None),
            P(),
            P(),
            P("grid", "comp", None, None),
            P("grid", "comp", None),
            P("grid", "comp", None),
        ),
        out_specs=P("grid", "comp", None),
        check_vma=False,
    )
```

```python
import functools
import math

import jax
import jax.numpy as jnp
import numpy as np
from jax import lax
from jax.experimental import pallas as pl
from jax.experimental.pallas import tpu as pltpu
from jax.sharding import PartitionSpec as P

ND = 36
NF = 32
LX = 128
STEPS = 2


def padded_2(array, sides, width):
    for axis, dim in sides:
        peers, length = (lax.axis_size(axis), array.shape[dim])
        up = [(i, (i + 1) % peers) for i in range(peers - 1)]
        down = [(j, i) for i, j in up]
        last = lax.slice_in_dim(array, length - width, length, axis=dim)
        initial = lax.slice_in_dim(array, 0, width, axis=dim)
        before = lax.ppermute(last, axis, up)
        after = lax.ppermute(initial, axis, down)
        array = jnp.concatenate([before, array, after], axis=dim)
    return array


def courant(comp_index, speed_row):
    direction = comp_index // NF
    frequency = comp_index % NF
    heading = 2.0 * math.pi * direction.astype(jnp.float32) / ND
    onehot_table = (frequency[:, None] == jnp.arange(NF, dtype=jnp.int32)[None, :]).astype(
        jnp.float32
    )
    celerity = jnp.sum(onehot_table * speed_row[None, :], axis=1)
    return (celerity * jnp.cos(heading), celerity * jnp.sin(heading))


def sweep_columns(values, number):
    padded = jnp.pad(values, ((0, 0), (0, 0), (1, 1)))
    forward = padded[:, :, 2:]
    behind = padded[:, :, :-2]
    return (
        values
        - 0.5 * number * (forward - behind)
        + 0.5 * number * number * (forward - 2.0 * values + behind)
    )


def sweep_rows(values, number):
    padded = jnp.pad(values, ((0, 0), (1, 1), (0, 0)))
    forward = padded[:, 2:, :]
    behind = padded[:, :-2, :]
    return (
        values
        - 0.5 * number * (forward - behind)
        + 0.5 * number * number * (forward - 2.0 * values + behind)
    )


def propagate(spectra, sea_float, courant_x, courant_y):
    count = spectra.shape[0]
    values = spectra.astype(jnp.float32).reshape(count, -1, LX)
    land_sea = sea_float.reshape(1, -1, LX)
    values = sweep_columns(values, courant_x[:, None, None]) * land_sea
    values = sweep_rows(values, courant_y[:, None, None]) * land_sea
    return values.reshape(count, -1).astype(jnp.bfloat16)


def advect_block(points, sea_rows, courant_x, courant_y):
    count = points.shape[0]
    values = points.reshape(count, -1, LX)
    extended = padded_2(values, (("comp", 1),), 1)
    widened = extended.astype(jnp.float32)
    widened = sweep_columns(widened, courant_x[:, None, None]) * sea_rows[None]
    widened = sweep_rows(widened, courant_y[:, None, None]) * sea_rows[None]
    return widened[:, 1:-1, :].reshape(count, -1).astype(jnp.bfloat16)


def source(points, sea_part, coupling_a, coupling_b):
    first_term = jnp.dot(coupling_a, points, preferred_element_type=jnp.float32)
    second = jnp.dot(coupling_b, points, preferred_element_type=jnp.float32)
    return (
        points.astype(jnp.float32) + 0.5 * sea_part[None, :] * first_term * jnp.tanh(second)
    ).astype(jnp.bfloat16)


def average(updated, received, targets, weights):
    count = updated.shape[1]
    hits = targets[:, None] == jnp.arange(count, dtype=jnp.int32)[None, :]
    weighted = (received.astype(jnp.float32) * weights[:, None]).astype(jnp.bfloat16)
    onehot_table = hits.astype(jnp.bfloat16)
    gathered_sum = lax.dot_general(
        weighted, onehot_table, (((0,), (0,)), ((), ())), preferred_element_type=jnp.float32
    )
    numerator = updated.astype(jnp.float32) + gathered_sum
    denominator = 1.0 + jnp.sum(hits.astype(jnp.float32) * weights[:, None], axis=0)
    return (numerator / denominator[None, :]).astype(jnp.bfloat16)


def share_intersection(updated, targets, groups, total_comps, my_grid):
    outgoing = jnp.take(updated, targets, axis=1).T.reshape(groups, -1, total_comps)
    everything = lax.all_gather(outgoing, "grid", axis=0, tiled=True)
    received = lax.dynamic_index_in_dim(
        everything.reshape(groups, groups, -1, total_comps), my_grid, 1, keepdims=False
    )
    return received.reshape(-1, total_comps)


def local(spectrum, sea_mask, speed, coupling_a, coupling_b, send_index, recv_index, recv_weight):
    local_comps = spectrum.shape[1]
    columns = spectrum.shape[2]
    groups = lax.axis_size("grid")
    pieces = lax.axis_size("comp")
    block_len = columns // pieces
    total_comps = coupling_a.shape[0]
    comp_index = lax.axis_index("comp") * local_comps + jnp.arange(local_comps, dtype=jnp.int32)
    courant_x, courant_y = courant(comp_index, speed[0])
    sea_float = sea_mask[0].astype(jnp.float32)
    sea_part = lax.dynamic_slice_in_dim(sea_float, lax.axis_index("comp") * block_len, block_len)
    targets = send_index.reshape(-1)
    my_grid = lax.axis_index("grid")
    spectra = spectrum[0]
    full_x, full_y = courant(jnp.arange(total_comps, dtype=jnp.int32), speed[0])
    block_rows = block_len // LX
    padded_sea = jnp.pad(sea_float.reshape(-1, LX), ((1, 1), (0, 0)))
    sea_rows = lax.dynamic_slice_in_dim(
        padded_sea, lax.axis_index("comp") * block_rows, block_rows + 2, 0
    )
    advected = propagate(spectra, sea_float, courant_x, courant_y)
    points = lax.all_to_all(advected, "comp", split_axis=1, concat_axis=0, tiled=True)
    for turn_index in range(STEPS):
        if turn_index > 0:
            points = advect_block(points, sea_rows, full_x, full_y)
        updated = source(points, sea_part, coupling_a, coupling_b)
        received = share_intersection(updated, targets, groups, total_comps, my_grid)
        points = average(updated, received, recv_index[0, 0], recv_weight[0, 0])
    spectra = lax.all_to_all(points, "comp", split_axis=0, concat_axis=1, tiled=True)
    return spectra[None]


MESH = pl.DeviceIdType.MESH
SUB = 16


def coefficients(number):
    square = number * number
    return (1.0 - square, 0.5 * (square - number), 0.5 * (square + number))


def flipped(index, mask, count):
    total = 0
    bit = 1
    while bit < count:
        total = total + lax.rem(index // bit + (mask // bit) % 2, 2) * bit
        bit *= 2
    return total


def wave_kernel(
    sizes,
    spec_hbm,
    sea_ref,
    speed_ref,
    turn_ref,
    a_hbm,
    b_hbm,
    send_ref,
    recv_ref,
    weight_ref,
    out_ref,
    spec_ref,
    celerity,
    a_ref,
    b_ref,
    table,
    local_table,
    outbox,
    field,
    updated,
    averaged,
    final,
    halo,
    pick_table,
    place_table,
    inverse,
    weight,
    picked,
    received,
    scaled,
    load_sem,
    first_send,
    first_recv,
    share_send,
    share_recv,
    halo_send,
    halo_recv,
    last_send,
    last_recv,
):
    pieces, groups, own, total, rows, slots = sizes
    block_len = rows * LX
    pairs = rows // 2
    me = lax.axis_index("comp")
    my_grid = lax.axis_index("grid")

    load_a = pltpu.make_async_copy(a_hbm, a_ref, load_sem.at[0])
    load_b = pltpu.make_async_copy(b_hbm, b_ref, load_sem.at[1])
    load_spec = pltpu.make_async_copy(spec_hbm, spec_ref, load_sem.at[2])
    load_spec.start()

    barrier = pltpu.get_barrier_semaphore()
    for mask in range(1, pieces):
        pl.semaphore_signal(
            barrier,
            inc=1,
            device_id={"comp": flipped(me, mask, pieces)},
            device_id_type=MESH,
        )
    for shift in range(1, groups):
        pl.semaphore_signal(
            barrier,
            inc=1,
            device_id={"grid": lax.rem(my_grid + shift, groups)},
            device_id_type=MESH,
        )

    lane = lax.broadcasted_iota(jnp.int32, (SUB, LX), 1)

    def upright(row):
        length = row.shape[1]
        across = lax.broadcasted_iota(jnp.int32, (length, length), 1)
        down = lax.broadcasted_iota(jnp.int32, (length, length), 0)
        square = jnp.broadcast_to(row.astype(jnp.float32), (length, length))
        return jnp.sum(jnp.where(across == down, square, 0.0), axis=1, keepdims=True)

    celerity[...] = jnp.broadcast_to(upright(speed_ref[...]), celerity.shape)

    def fill(source_row, target, target_row):
        part = pl.multiple_of(lax.rem(source_row, NF), SUB)
        pace = celerity[pl.ds(part, SUB), :]
        cx = pace * turn_ref[0, source_row // NF]
        cy = pace * turn_ref[1, source_row // NF]
        x0, xp, xm = coefficients(cx)
        y0, yp, ym = coefficients(cy)
        here = pl.ds(target_row, SUB)
        target[0, here, :] = x0
        target[1, here, :] = jnp.where(lane == LX - 1, 0.0, xp)
        target[2, here, :] = jnp.where(lane == 0, 0.0, xm)
        target[3, here, :] = y0
        target[4, here, :] = yp
        target[5, here, :] = ym

    def fill_local(step, carry):
        fill(
            pl.multiple_of(me * own + step * SUB, SUB),
            local_table,
            pl.multiple_of(step * SUB, SUB),
        )
        return carry

    lax.fori_loop(0, own // SUB, fill_local, 0)

    def swept(value, sea, coefs):
        return (
            coefs[0] * value
            + coefs[1] * pltpu.roll(value, LX - 1, 1)
            + coefs[2] * pltpu.roll(value, 1, 1)
        ) * sea

    def crossed(middle, above, below, sea, coefs):
        return ((coefs[3] * middle + coefs[4] * above + coefs[5] * below) * sea).astype(
            jnp.bfloat16
        )

    lattice_rows = pieces * rows
    load_spec.wait()
    load_a.start()
    load_b.start()

    def sea_line(row):
        inside = jnp.minimum(jnp.maximum(row, 0), lattice_rows - 1)
        line = sea_ref[:, pl.ds(pl.multiple_of(inside * LX, LX), LX)]
        return jnp.where(inside == row, line, 0).astype(jnp.float32)

    def advect_first(peer, pair, store):
        base = peer * rows + 2 * pair
        where_rows = [
            jnp.minimum(jnp.maximum(base - 1 + t, 0), lattice_rows - 1) for t in range(4)
        ]
        seas = [sea_line(base - 1 + t) for t in range(4)]

        def step(block, carry):
            here = pl.ds(pl.multiple_of(block * SUB, SUB), SUB)
            coefs = [local_table[i, here, :] for i in range(6)]
            lines = [
                swept(
                    spec_ref[here, pl.ds(pl.multiple_of(row * LX, LX), LX)].astype(jnp.float32),
                    seas[t],
                    coefs,
                )
                for t, row in enumerate(where_rows)
            ]
            for t in range(2):
                store(t, block, crossed(lines[t + 1], lines[t + 2], lines[t], seas[t + 1], coefs))
            return carry

        lax.fori_loop(0, own // SUB, step, 0, unroll=9)

    order = list(range(pieces - 1, 0, -1))
    mine = pl.ds(pl.multiple_of(me * own, SUB), own)

    def first_copy(pair, mask):
        return pltpu.make_async_remote_copy(
            src_ref=outbox.at[pair, mask],
            dst_ref=field.at[pl.ds(2 * pair, 2), mine, :],
            send_sem=first_send.at[pair, mask],
            recv_sem=first_recv.at[pair, mask],
            device_id={"comp": flipped(me, mask, pieces)},
            device_id_type=MESH,
        )

    for pair in range(pairs):
        for mask in order:

            def store_out(t, block, value, pair=pair, mask=mask):
                here = pl.ds(pl.multiple_of(block * SUB, SUB), SUB)
                outbox[pair, mask, t, here, :] = value

            advect_first(flipped(me, mask, pieces), pair, store_out)
            if pair == 0 and mask == order[0]:
                pl.semaphore_wait(barrier, pieces - 1 + groups - 1)
            first_copy(pair, mask).start()

    for pair in range(pairs):

        def store_own(t, block, value, pair=pair):
            here = pl.ds(pl.multiple_of(me * own + block * SUB, SUB), SUB)
            field[2 * pair + t, here, :] = value

        advect_first(me, pair, store_own)

    def fill_all(step, carry):
        row = pl.multiple_of(step * SUB, SUB)
        fill(row, table, row)
        return carry

    lax.fori_loop(0, total // SUB, fill_all, 0)

    places = groups * slots
    point = lax.broadcasted_iota(jnp.int32, (places, block_len), 1)
    spot = lax.broadcasted_iota(jnp.int32, (slots, block_len), 1).astype(jnp.float32)
    for group in range(groups):
        wanted = upright(send_ref[group : group + 1, :]) == spot
        pick_table[group * slots : (group + 1) * slots, :] = wanted.astype(jnp.float32).astype(
            jnp.bfloat16
        )
    hits = (upright(recv_ref[...]) == point.astype(jnp.float32)).astype(jnp.float32)
    place_table[...] = hits.astype(jnp.bfloat16)
    weight[...] = upright(weight_ref[...])
    inverse[...] = 1.0 / (1.0 + jnp.sum(hits * weight[...], axis=0, keepdims=True))

    @pl.when(me == 0)
    def _():
        halo[0] = jnp.zeros_like(halo[0])

    @pl.when(me == pieces - 1)
    def _():
        halo[1] = jnp.zeros_like(halo[1])

    load_a.wait()
    load_b.wait()

    tall = total

    def source_rows(one, two):
        half = 0.5 * jnp.concatenate(
            [sea_line(me * rows + one), sea_line(me * rows + two)], axis=1
        )

        def step(index, carry):
            here = pl.ds(pl.multiple_of(index * tall, SUB), tall)
            values = jnp.concatenate([field[one], field[two]], axis=1)
            first = jnp.dot(a_ref[here, :], values, preferred_element_type=jnp.float32)
            second = jnp.dot(b_ref[here, :], values, preferred_element_type=jnp.float32)
            own_values = jnp.concatenate([field[one, here, :], field[two, here, :]], axis=1)
            result = (own_values.astype(jnp.float32) + half * first * jnp.tanh(second)).astype(
                jnp.bfloat16
            )
            updated[one, here, :] = result[:, :LX]
            updated[two, here, :] = result[:, LX:]
            return carry

        lax.fori_loop(0, total // tall, step, 0)

    def share_copy(turn, shift):
        peer = lax.rem(my_grid + shift, groups)
        return pltpu.make_async_remote_copy(
            src_ref=picked.at[pl.ds(pl.multiple_of(peer * slots, SUB), slots), :],
            dst_ref=received.at[turn, pl.ds(pl.multiple_of(my_grid * slots, SUB), slots), :],
            send_sem=share_send.at[turn, shift],
            recv_sem=share_recv.at[turn, shift],
            device_id={"grid": peer},
            device_id_type=MESH,
        )

    def share(turn):
        everything = jnp.concatenate([updated[r] for r in range(rows)], axis=1)
        chosen = lax.dot_general(
            pick_table[...],
            everything,
            (((1,), (1,)), ((), ())),
            preferred_element_type=jnp.float32,
        )
        picked[...] = chosen.astype(jnp.bfloat16)
        for shift in range(1, groups):
            share_copy(turn, shift).start()
        here = pl.ds(pl.multiple_of(my_grid * slots, SUB), slots)
        received[turn, here, :] = picked[here, :]
        for shift in range(1, groups):
            share_copy(turn, shift).wait()
        scaled[...] = (
            (received[turn].astype(jnp.float32) * weight[...])
            .astype(jnp.bfloat16)
            .astype(jnp.float32)
            .T.astype(jnp.bfloat16)
        )

    def average_rows(here, wanted, store):
        for row in wanted:
            columns = slice(row * LX, (row + 1) * LX)
            added = jnp.dot(
                scaled[here, :], place_table[:, columns], preferred_element_type=jnp.float32
            )
            value = (updated[row, here, :].astype(jnp.float32) + added) * inverse[:, columns]
            store(row, value.astype(jnp.bfloat16))

    def halo_up():
        return pltpu.make_async_remote_copy(
            src_ref=averaged.at[rows - 1],
            dst_ref=halo.at[0],
            send_sem=halo_send.at[0],
            recv_sem=halo_recv.at[0],
            device_id={"comp": jnp.minimum(me + 1, pieces - 1)},
            device_id_type=MESH,
        )

    def halo_down():
        return pltpu.make_async_remote_copy(
            src_ref=averaged.at[0],
            dst_ref=halo.at[1],
            send_sem=halo_send.at[1],
            recv_sem=halo_recv.at[1],
            device_id={"comp": jnp.maximum(me - 1, 0)},
            device_id_type=MESH,
        )

    def advect_rows(wanted):
        seas = {row: sea_line(me * rows + row) for row in range(-1, rows + 1)}

        def step(block, carry):
            here = pl.ds(pl.multiple_of(block * SUB, SUB), SUB)
            coefs = [table[i, here, :] for i in range(6)]
            lines = {}

            def line(row):
                if row not in lines:
                    if row < 0:
                        raw = halo[0, here, :]
                    elif row >= rows:
                        raw = halo[1, here, :]
                    else:
                        raw = averaged[row, here, :]
                    lines[row] = swept(raw.astype(jnp.float32), seas[row], coefs)
                return lines[row]

            for row in wanted:
                field[row, here, :] = crossed(
                    line(row), line(row + 1), line(row - 1), seas[row], coefs
                )
            return carry

        lax.fori_loop(0, total // SUB, step, 0, unroll=12)

    for pair in range(pairs):
        for mask in order:
            first_copy(pair, mask).wait_recv()
        source_rows(2 * pair, 2 * pair + 1)
    for pair in range(pairs):
        for mask in order:
            first_copy(pair, mask).wait_send()

    inner = list(range(1, rows - 1))
    whole = pl.ds(0, total)
    for turn in range(STEPS):
        if turn > 0:

            def average_step(index, carry, wanted):
                here = pl.ds(pl.multiple_of(index * own, SUB), own)

                def store_row(row, value):
                    averaged[row, here, :] = value

                average_rows(here, wanted, store_row)
                return carry

            lax.fori_loop(
                0, total // own, functools.partial(average_step, wanted=(0, rows - 1)), 0
            )

            @pl.when(me < pieces - 1)
            def _():
                halo_up().start()

            @pl.when(me > 0)
            def _():
                halo_down().start()

            lax.fori_loop(0, total // own, functools.partial(average_step, wanted=inner), 0)
            advect_rows(inner)
            for pair in range(len(inner) // 2):
                source_rows(inner[2 * pair], inner[2 * pair + 1])

            @pl.when(me < pieces - 1)
            def _():
                halo_up().wait_send()
                halo_down().wait_recv()

            @pl.when(me > 0)
            def _():
                halo_down().wait_send()
                halo_up().wait_recv()

            advect_rows((0, rows - 1))
            source_rows(0, rows - 1)
        share(turn)

    def block_rows(peer):
        return pl.ds(pl.multiple_of(peer * own, SUB), own)

    my_points = pl.multiple_of(me * block_len, LX)

    def last_copy(mask):
        peer = flipped(me, mask, pieces)
        return pltpu.make_async_remote_copy(
            src_ref=final.at[block_rows(peer), :],
            dst_ref=out_ref.at[:, pl.ds(my_points, block_len)],
            send_sem=last_send.at[mask],
            recv_sem=last_recv.at[mask],
            device_id={"comp": peer},
            device_id_type=MESH,
        )

    for mask in order:
        here = block_rows(flipped(me, mask, pieces))

        def store_final(row, value, here=here):
            final[here, row * LX : (row + 1) * LX] = value

        average_rows(here, range(rows), store_final)
        last_copy(mask).start()

    def store_mine(row, value):
        out_ref[:, pl.ds(pl.multiple_of(my_points + row * LX, LX), LX)] = value

    average_rows(mine, range(rows), store_mine)
    for mask in order:
        last_copy(mask).wait()


def fused(spectrum, sea_mask, speed, coupling_a, coupling_b, send_index, recv_index, recv_weight):
    own, columns = spectrum.shape[1:]
    pieces = lax.axis_size("comp")
    groups = lax.axis_size("grid")
    total = coupling_a.shape[0]
    rows = columns // pieces // LX
    slots = send_index.shape[-1]
    places = groups * slots
    heading = (2.0 * math.pi / ND) * np.arange(total // NF)
    turns = np.stack([np.cos(heading), np.sin(heading)]).astype(np.float32)
    vmem = pl.BlockSpec(memory_space=pltpu.VMEM)
    anywhere = pl.BlockSpec(memory_space=pltpu.HBM)
    half = jnp.bfloat16
    dma = pltpu.SemaphoreType.DMA
    smem = pl.BlockSpec(memory_space=pltpu.SMEM)
    lines = pl.pallas_call(
        functools.partial(wave_kernel, (pieces, groups, own, total, rows, slots)),
        out_shape=jax.ShapeDtypeStruct((own, columns), half),
        in_specs=[anywhere, vmem, vmem, smem, anywhere, anywhere, vmem, vmem, vmem],
        out_specs=vmem,
        scratch_shapes=[
            pltpu.VMEM((own, columns), half),
            pltpu.VMEM((NF, LX), jnp.float32),
            pltpu.VMEM(coupling_a.shape, half),
            pltpu.VMEM(coupling_b.shape, half),
            pltpu.VMEM((6, total, LX), jnp.float32),
            pltpu.VMEM((6, own, LX), jnp.float32),
            pltpu.VMEM((rows // 2, pieces, 2, own, LX), half),
            pltpu.VMEM((rows, total, LX), half),
            pltpu.VMEM((rows, total, LX), half),
            pltpu.VMEM((rows, total, LX), half),
            pltpu.VMEM((total, rows * LX), half),
            pltpu.VMEM((2, total, LX), half),
            pltpu.VMEM((places, rows * LX), half),
            pltpu.VMEM((places, rows * LX), half),
            pltpu.VMEM((1, rows * LX), jnp.float32),
            pltpu.VMEM((places, 1), jnp.float32),
            pltpu.VMEM((places, total), half),
            pltpu.VMEM((STEPS, places, total), half),
            pltpu.VMEM((total, places), half),
            dma((3,)),
            dma((rows // 2, pieces)),
            dma((rows // 2, pieces)),
            dma((STEPS, groups)),
            dma((STEPS, groups)),
            dma((2,)),
            dma((2,)),
            dma((pieces,)),
            dma((pieces,)),
        ],
        compiler_params=pltpu.CompilerParams(
            collective_id=0, has_side_effects=True, vmem_limit_bytes=64900000
        ),
        name="wave_steps",
    )(
        spectrum[0],
        sea_mask,
        speed,
        jnp.asarray(turns),
        coupling_a,
        coupling_b,
        send_index[0, 0],
        recv_index[0],
        recv_weight[0],
    )
    return lines[None]


def fits(pieces, groups, own, rows, slots):
    power = pieces & (pieces - 1) == 0
    return power and own % SUB == 0 and rows % 2 == 0 and rows >= 4 and slots % SUB == 0


def program(spectrum, sea_mask, speed, coupling_a, coupling_b, send_index, recv_index, recv_weight):
    pieces = lax.axis_size("comp")
    groups = lax.axis_size("grid")
    rows = spectrum.shape[2] // pieces // LX
    whole = rows * pieces * LX == spectrum.shape[2]
    chosen = local
    if whole and fits(pieces, groups, spectrum.shape[1], rows, send_index.shape[-1]):
        chosen = fused
    return chosen(
        spectrum, sea_mask, speed, coupling_a, coupling_b, send_index, recv_index, recv_weight
    )


def solution(mesh):
    return jax.shard_map(
        program,
        mesh=mesh,
        in_specs=(
            P("grid", "comp", None),
            P("grid", None),
            P("grid", None),
            P(),
            P(),
            P("grid", "comp", None, None),
            P("grid", "comp", None),
            P("grid", "comp", None),
        ),
        out_specs=P("grid", "comp", None),
        check_vma=False,
    )
```
